32 devices in a mesh: seq: 8 (over y, x, core), trunk: 4 (over z).
Axes of the slice: x: 2, y: 2, z: 4, core: 2. Of those that a mesh axis runs over, the one named last changes fastest.
Arguments:
- tokens: int32 [8, 131072], P('seq', 'trunk'), may hold values from 0 to 3
- first_weight: bfloat16 [128, 768], replicated, may hold values from -1 to 1
- second_weight: bfloat16 [1536, 1024], replicated, may hold values from -0.15625 to 0.15625
- third_weight: bfloat16 [2048, 1536], replicated, may hold values from -0.125 to 0.125
- norm_gain: float32 [1536], replicated, may hold values from 0.1 to 1.9
- query_weight: bfloat16 [1536, 1024], replicated, may hold values from -0.15625 to 0.15625
- context_weight: bfloat16 [1536, 320], replicated, may hold values from -0.15625 to 0.15625
- output_weight: bfloat16 [1536, 1536], replicated, may hold values from -0.15625 to 0.15625
- pair_bias: float32 [8, 8, 64, 64], P('seq', None, 'trunk'), may hold values from -6 to 300
- cotangent: bfloat16 [8, 1024, 1536], P('seq', 'trunk'), may hold values from -6 to 6
Outputs:
- encoded: bfloat16 [8, 1024, 1536], P('seq', 'trunk')
- update: bfloat16 [8, 1024, 1536], P('seq', 'trunk')
- input_gradient: bfloat16 [8, 1024, 1536], P('seq', 'trunk')
- query_gradient: float32 [1536, 1024], P(('seq', 'trunk'))
- context_gradient: float32 [1536, 320], P(('seq', 'trunk'))
- output_gradient: float32 [1536, 1536], P(('seq', 'trunk'))
The draws below stay inside these ranges and needn't reach their ends.
All inputs are finite; a program needn't handle non-finite values.
Results may differ from the reference program's by a relative error of at most 0.019.
Values may be sent and summed in bfloat16 or wider, within the bound.
A program may use at most 384 MiB of HBM per device.

```python
import math
import jax
import jax.numpy as jnp
from jax import lax

D = 1536
HEADS = 8
DK = 128
DV = 192
C1 = 768
C2 = 1024
PATCH = 32
PAIR = 16
TR = 256
SAMPLES = 8
LT = 1024
N_TRUNK = 4


def draw_pair_bias(key, part):
    blocks = TR * N_TRUNK // PAIR
    bias_shape = (SAMPLES, HEADS, blocks, blocks)
    key_base = jax.random.fold_in(key, 0)
    biases = jnp.clip(1.5 * jax.random.normal(key_base, bias_shape, jnp.float32), -6.0, 6.0)
    return biases


def touch_ends(entries, stream_key, least, high):
    longest = entries.shape.index(max(entries.shape))
    spots = []
    for shift in (0, 1):
        where = [jax.random.randint(jax.random.fold_in(stream_key, axis), (), 0, length) for axis, length in enumerate(entries.shape)]
        where[longest] = (where[longest] + shift) % entries.shape[longest]
        spots.append(tuple(where))
    return entries.at[spots[0]].set(least).at[spots[1]].set(high)


def block_levels(stream_key, shape, shards, low, high):
    level = 1.0
    for position, blocks in shards:
        steps = jax.random.uniform(jax.random.fold_in(jax.random.fold_in(stream_key, 6), position), (blocks,), jnp.float32, low / len(shards), high / len(shards))
        level = level * jnp.repeat(jnp.exp(steps), shape[position] // blocks).reshape((-1,) + (1,) * (len(shape) - 1 - position))
    return level


def normal_values(own_key, extent, spread, limit, pieces=(), kind=jnp.bfloat16):
    gain = block_levels(own_key, extent, pieces, -0.22, 0.18) if pieces else 1.0
    entries = jax.random.normal(own_key, extent, jnp.float32) * spread * gain
    return jnp.minimum(jnp.maximum(entries, -limit), limit).astype(kind)


def setup_inputs(seed: int = 0) -> dict:
    key_of = jax.random.split(jax.random.key(seed), 11)
    tokens = touch_ends(jax.random.randint(key_of[0], (SAMPLES, LT * PATCH * 4), 0, 4), jax.random.fold_in(key_of[0], 1), 0, 3).astype(jnp.int32)
    first_weight = normal_values(key_of[1], (4 * PATCH, C1), PATCH ** -0.5, 1.0)
    second_weight = normal_values(key_of[2], (2 * C1, C2), (2 * C1) ** -0.5, 0.15625)
    third_weight = normal_values(key_of[3], (2 * C2, D), (2 * C2) ** -0.5, 0.125)
    norm_gain = jnp.clip(1.0 + 0.18 * jax.random.normal(key_of[4], (D,), jnp.float32), 0.1, 1.9)
    query_weight = normal_values(key_of[5], (D, HEADS * DK), D ** -0.5, 0.15625)
    context_weight = normal_values(key_of[6], (D, DK + DV), D ** -0.5, 0.15625)
    output_weight = normal_values(key_of[7], (HEADS * DV, D), (HEADS * DV) ** -0.5, 0.15625)
    pair_bias = draw_pair_bias(jax.random.fold_in(key_of[10], 71), 0)
    cotangent = normal_values(key_of[9], (SAMPLES, LT, D), 1.0, 6.0, ((0, 8), (1, 4)))
    return {"tokens": tokens, "first_weight": first_weight, "second_weight": second_weight, "third_weight": third_weight, "norm_gain": norm_gain, "query_weight": query_weight, "context_weight": context_weight, "output_weight": output_weight, "pair_bias": pair_bias, "cotangent": cotangent}


EPS = 1e-06

def encode(tokens, first_weight, second_weight, third_weight):
    leading = tokens.shape[:-1]
    onehot = jax.nn.one_hot(tokens, 4, dtype=jnp.bfloat16)
    patches = onehot.reshape(-1, first_weight.shape[0])
    section_one = jax.nn.gelu(jnp.dot(patches, first_weight, preferred_element_type=jnp.float32)).astype(jnp.bfloat16)
    section_two = jax.nn.gelu(jnp.dot(section_one.reshape(-1, second_weight.shape[0]), second_weight, preferred_element_type=jnp.float32)).astype(jnp.bfloat16)
    encoded = jnp.dot(section_two.reshape(-1, third_weight.shape[0]), third_weight, preferred_element_type=jnp.float32).astype(jnp.bfloat16)
    row_count = tokens.shape[-1] * 4 // first_weight.shape[0] // 4
    return encoded.reshape(leading + (row_count, third_weight.shape[1]))

def add_bias(scores, biases):
    head_count, row_total, col_total = scores.shape
    blocks = scores.reshape(head_count, row_total // PAIR, PAIR, col_total // PAIR, PAIR)
    return (blocks + biases[:, :, None, :, None]).reshape(head_count, row_total, col_total)

def trunk_sample(trunk_in, norm_gain, query_weight, context_weight, output_weight, biases, cot_rows):
    inputs = trunk_in.astype(jnp.float32)
    inverse = lax.rsqrt(lax.optimization_barrier(jnp.mean(inputs * inputs, axis=-1, keepdims=True)) + EPS)
    whitened = inputs * inverse
    gains = norm_gain.astype(jnp.float32)
    normed = (whitened * gains).astype(jnp.bfloat16)
    row_total = trunk_in.shape[0]
    queries = jnp.dot(normed, query_weight, preferred_element_type=jnp.float32).astype(jnp.bfloat16)
    context = jnp.dot(normed, context_weight, preferred_element_type=jnp.float32).astype(jnp.bfloat16)
    key_rows = context[:, :DK].astype(jnp.float32)
    value_rows = context[:, DK:].astype(jnp.float32)
    score_scale = 1.0 / math.sqrt(DK)
    query_heads = queries.reshape(row_total, HEADS, DK).astype(jnp.float32)
    scores = jnp.einsum('qhd,kd->hqk', query_heads, key_rows) * score_scale
    scores = add_bias(scores, biases)
    shifted = jnp.exp(scores - lax.optimization_barrier(jnp.max(scores, axis=-1, keepdims=True)))
    soft = shifted / lax.optimization_barrier(jnp.sum(shifted, axis=-1, keepdims=True))
    soft_rounded = soft.astype(jnp.bfloat16)
    soft_wide = soft_rounded.astype(jnp.float32)
    mixture = jnp.einsum('hqk,kv->qhv', soft_wide, value_rows).reshape(row_total, HEADS * DV).astype(jnp.bfloat16)
    update = jnp.dot(mixture, output_weight, preferred_element_type=jnp.float32).astype(jnp.bfloat16)
    grad_mix = jnp.dot(cot_rows, output_weight.T, preferred_element_type=jnp.float32).astype(jnp.bfloat16)
    mix_heads = grad_mix.reshape(row_total, HEADS, DV).astype(jnp.float32)
    grad_soft = jnp.einsum('qhv,kv->hqk', mix_heads, value_rows)
    row_delta = lax.optimization_barrier(jnp.sum(soft * grad_soft, axis=-1, keepdims=True))
    grad_score = (soft * (grad_soft - row_delta)).astype(jnp.bfloat16)
    score_wide = grad_score.astype(jnp.float32)
    grad_queries = (jnp.einsum('hqk,kd->qhd', score_wide, key_rows) * score_scale).reshape(row_total, HEADS * DK).astype(jnp.bfloat16)
    grad_keys = jnp.einsum('hqk,qhd->kd', score_wide, query_heads) * score_scale
    grad_values = jnp.einsum('hqk,qhv->kv', soft_wide, mix_heads)
    grad_context = jnp.concatenate([grad_keys, grad_values], axis=-1).astype(jnp.bfloat16)
    grad_normed = jnp.dot(grad_queries, query_weight.T, preferred_element_type=jnp.float32) + jnp.dot(grad_context, context_weight.T, preferred_element_type=jnp.float32)
    grad_white = grad_normed * gains
    input_gradient = (inverse * (grad_white - whitened * lax.optimization_barrier(jnp.mean(grad_white * whitened, axis=-1, keepdims=True)))).astype(jnp.bfloat16)
    query_term = jnp.dot(normed.T, grad_queries, preferred_element_type=jnp.float32)
    context_term = jnp.dot(normed.T, grad_context, preferred_element_type=jnp.float32)
    output_term = jnp.dot(mixture.T, cot_rows, preferred_element_type=jnp.float32)
    return (update, input_gradient, query_term, context_term, output_term)

def reference(tokens, first_weight, second_weight, third_weight, norm_gain, query_weight, context_weight, output_weight, pair_bias, cotangent):
    encoded = encode(tokens, first_weight, second_weight, third_weight)

    def per_sample(totals, sample_in):
        rows_in, biases, cot_rows = sample_in
        update, input_gradient, query_term, context_term, output_term = trunk_sample(rows_in, norm_gain, query_weight, context_weight, output_weight, biases, cot_rows)
        return ((totals[0] + query_term, totals[1] + context_term, totals[2] + output_term), (update, input_gradient))
    initial = (jnp.zeros((D, HEADS * DK), jnp.float32), jnp.zeros((D, DK + DV), jnp.float32), jnp.zeros((HEADS * DV, D), jnp.float32))
    totals, outputs = lax.scan(per_sample, initial, (encoded, pair_bias, cotangent))
    factor = 1.0 / math.sqrt(SAMPLES * TR * N_TRUNK)
    return (encoded, outputs[0], outputs[1], totals[0] * factor, totals[1] * factor, totals[2] * factor)
```

```python
import functools
import math

import jax
import jax.numpy as jnp
from jax import lax
from jax.experimental import pallas as pl
from jax.experimental.pallas import tpu as pltpu
from jax.sharding import PartitionSpec as P

HEADS = 8
DK = 128
DV = 192
PAIR = 16
EPS = 1e-06
F32 = jnp.float32
BF16 = jnp.bfloat16
MESH = pl.DeviceIdType.MESH


def dot_on(a, b, da, db):
    return lax.dot_general(a, b, (((da,), (db,)), ((), ())), preferred_element_type=F32)


def bits_of(size):
    return [1 << e for e in range(size.bit_length() - 1)]


def flip(index, mask):
    out = index
    bit = 1
    while bit <= mask:
        if mask & bit:
            out = out + bit - 2 * bit * ((index // bit) % 2)
        bit *= 2
    return out


def spans(bits):
    masks = [0]
    for bit in bits:
        masks = masks + [m | bit for m in masks]
    return masks


def seq_orders(n):
    ups = [b for b in bits_of(n) if b > 1]
    return ups + [1], ups[::-1] + [1]


def kernel(
    n, nt, tok_h, w1_h, w2_h, w3_h, gain_h, wq_h, wc_h, wo_h, bias_h, cot_h,
    enc_o, upd_o, inp_o, qg_o, cg_o, og_o, cot,
    tok, w1, w2, w3, gain, wc, bias,
    enc, nrm, nrt, nbk, q, gt, ctx, kaug, kt, vaug, vt, pt, linv, mixt, mixf, mbk,
    cbuf, gqt, gcx, dkp, ost, qst, cst, zs_d, zr_d, zs_o, zr_o, zs_q, zr_q, zs_c, zr_c,
    qg, cg, og,
    in_sem, out_sem, c_sem, cot_s, cot_r, ctx_s, ctx_r, nb_s, nb_r, mb_s, mb_r,
    gq_s, gq_r, gc_s, gc_r, d_s, d_r, o_s, o_r, qz_s, qz_r, cz_s, cz_r,
):
    seq = lax.axis_index("seq")
    trunk = lax.axis_index("trunk")
    rows, width = enc.shape
    total = nt * rows
    blocks = bias.shape[2]
    scale = 1.0 / math.sqrt(DK)
    factor = 1.0 / math.sqrt(rows * nt * n)
    blk = width // n
    part = blk // nt
    orders = seq_orders(n)
    tbits = bits_of(nt)
    sends = []

    def load(i, src, dst):
        copy = pltpu.make_async_copy(src, dst, in_sem.at[i])
        copy.start()
        return copy

    def store(i, src, dst):
        copy = pltpu.make_async_copy(src, dst, out_sem.at[i])
        copy.start()
        return copy

    def push(axis, peer, src, dst, ssem, rsem):
        copy = pltpu.make_async_remote_copy(
            src_ref=src, dst_ref=dst, send_sem=ssem, recv_sem=rsem,
            device_id={axis: peer}, device_id_type=MESH,
        )
        copy.start()
        sends.append(copy)
        return copy

    half = rows // 2
    loads = {}
    pairs = (
        (tok_h, tok), (w1_h, w1), (w2_h, w2), (w3_h, w3), (gain_h, gain), (wc_h, wc),
        (bias_h, bias), (cot_h.reshape(2, half, width), cbuf.at[0]),
    )
    for i, (src, dst) in enumerate(pairs):
        loads[i] = load(i, src, dst)

    barrier = pltpu.get_barrier_semaphore()
    for m in range(1, n):
        pl.semaphore_signal(barrier, inc=1, device_id={"seq": flip(seq, m)}, device_id_type=MESH)
    for m in range(1, nt):
        pl.semaphore_signal(
            barrier, inc=1, device_id={"trunk": flip(trunk, m)}, device_id_type=MESH
        )
    pl.semaphore_wait(barrier, n - 1 + nt - 1)

    def gather_stage(buf, h, k, ssem, rsem, own=None):
        order = orders[h]
        if k >= len(order):
            return {}
        out = {}
        for m in spans(order[:k]):
            to = m ^ order[k]
            src = own if (own is not None and m == 0) else buf.at[m, h]
            out[to] = push(
                "seq", flip(seq, order[k]), src, buf.at[to, h], ssem.at[h, to], rsem.at[h, to]
            )
        return out

    def block(index):
        return pl.ds(pl.multiple_of(index * blk, 16), blk)

    def exchange(src, dst, ssem, rsem):
        out = {}
        for m in range(1, n):
            out[m] = push(
                "seq", flip(seq, m), src.at[block(flip(seq, m))], dst.at[m], ssem.at[m], rsem.at[m]
            )
        return out

    stages = len(orders[0])
    cot_w = [[None] * stages for _ in range(2)]

    def cot_stage(k):
        for h in range(2):
            own = cot_h.at[pl.ds(h * half, half)]
            cot_w[h][k] = gather_stage(cot, h, k, cot_s, cot_r, own=own)

    cot_stage(0)

    def settle(waits, k):
        for h in range(2):
            for copy in waits[h][k].values():
                copy.wait_recv()

    loads[0].wait()
    loads[1].wait()
    taps, c1 = w1.shape
    c2 = w2.shape[1]
    patch = taps // 4
    bases = tok[...].astype(F32).astype(BF16)
    base = lax.broadcasted_iota(jnp.int32, (4 * patch, taps), 0)
    lane = lax.broadcasted_iota(jnp.int32, (4 * patch, taps), 1)
    code = (lax.broadcasted_iota(jnp.int32, (rows, taps), 1) % 4).astype(F32)

    def section_one(k):
        spread = dot_on(bases, (lane // 4 + k * patch == base).astype(BF16), 1, 0)
        onehot = (spread == code).astype(BF16)
        return jax.nn.gelu(dot_on(onehot, w1[...], 1, 0)).astype(BF16)

    wide_part = dkp.shape[1]
    for j in range(2):
        left, right = section_one(2 * j), section_one(2 * j + 1)
        if j == 0:
            loads[2].wait()
        two = jax.nn.gelu(
            dot_on(left, w2[:c1, :], 1, 0) + dot_on(right, w2[c1:, :], 1, 0)
        ).astype(BF16)
        if j == 0:
            loads[3].wait()
        else:
            wq = w2
            loads[8] = load(8, wq_h, wq)
        term = dot_on(two, w3[j * c2 : (j + 1) * c2, :], 1, 0)
        for i in range(width // wide_part):
            cols = slice(i * wide_part, (i + 1) * wide_part)
            if j == 0:
                dkp[i * rows : (i + 1) * rows, :] = term[:, cols]
            else:
                enc[:, cols] = (dkp[i * rows : (i + 1) * rows, :] + term[:, cols]).astype(BF16)
    wo = w3.at[:width]
    loads[9] = load(9, wo_h, wo)
    stores = [store(0, enc, enc_o)]

    wide = enc[...].astype(F32)
    inverse = lax.rsqrt(jnp.mean(wide * wide, axis=-1, keepdims=True) + EPS)
    loads[4].wait()
    nrm[...] = (wide * inverse * gain[...].reshape(1, width)).astype(BF16)
    loads[5].wait()
    context = dot_on(nrm[...], wc[...], 1, 1).astype(BF16)

    def pack(keys, values):
        low, high = values[:half, 128:DV], values[half:rows, 128:DV]
        return keys, values[:, :128], jnp.concatenate([low, high], axis=1)

    for i, piece in enumerate(pack(context[:, :DK], context[:, DK:])):
        ctx[0, i * rows : i * rows + piece.shape[0], :] = piece
    ctx_w = {}
    torder = tbits[::-1]

    def ctx_send(m, bit):
        to = m ^ bit
        ctx_w[to] = push(
            "trunk", flip(trunk, bit), ctx.at[m], ctx.at[to], ctx_s.at[to], ctx_r.at[to]
        )

    for bit in torder:
        ctx_send(0, bit)
    settle(cot_w, 0)
    cot_stage(1)
    nrt[...] = nrm[...].T
    nb_w = exchange(nrt, nbk, nb_s, nb_r)

    loads[8].wait()
    qall = dot_on(nrm[...], wq[...], 1, 0).astype(BF16)
    loads[6].wait()
    lift = (
        lax.broadcasted_iota(jnp.int32, (rows, rows // PAIR), 0) // PAIR
        == lax.broadcasted_iota(jnp.int32, (rows, rows // PAIR), 1)
    ).astype(BF16)
    for head in range(HEADS):
        q[head, :, :DK] = qall[:, head * DK : (head + 1) * DK]
        b = bias[head] * math.sqrt(DK)
        top = b.astype(BF16)
        low = (b - top.astype(F32)).astype(BF16)
        both = jnp.concatenate([top, low], axis=1)
        q[head, :, DK:] = dot_on(lift, both, 1, 0).astype(BF16)
    relayed = set()
    for k in range(1, len(torder)):
        for m in spans(torder[:k]):
            if m & torder[k - 1]:
                ctx_w[m].wait_recv()
                relayed.add(m)
                for bit in torder[k:]:
                    ctx_send(m, bit)
    loads[7].wait()
    loads[9].wait()
    gt[...] = dot_on(wo[...], cbuf[0].reshape(rows, width), 1, 1).astype(BF16).reshape(gt.shape)
    for m in range(nt):
        if m and m not in relayed:
            ctx_w[m].wait_recv()
        keys = ctx[m, :rows, :]
        v0 = ctx[m, rows : 2 * rows, :]
        v1p = ctx[m, 2 * rows :, :]
        v1 = jnp.concatenate([v1p[:, :64], v1p[:, 64:]], axis=0)
        ones = (lax.broadcasted_iota(jnp.int32, (rows, 256 - DV), 1) < 2).astype(BF16)
        values = jnp.concatenate([v0, v1, ones], axis=1)
        at = flip(trunk, m) * (rows // PAIR)
        cell = lax.broadcasted_iota(jnp.int32, (rows, blocks), 0) // PAIR + at
        pick = (cell == lax.broadcasted_iota(jnp.int32, (rows, blocks), 1)).astype(BF16)
        kaug[m * rows : (m + 1) * rows, :] = jnp.concatenate([keys, pick, pick], axis=1)
        kt[:, m * rows : (m + 1) * rows] = keys.T
        vaug[m * rows : (m + 1) * rows, :] = values
        vt[:, m * rows : (m + 1) * rows] = values.T

    rate = scale * math.log2(math.e)

    def forward(head, carry):
        raw = dot_on(kaug[...], q[head], 1, 1)
        peak = jnp.max(raw, axis=0, keepdims=True)
        p = jnp.exp2((raw - peak) * rate).astype(BF16)
        pt[head] = p
        mixed = dot_on(vt[...], p, 1, 0)
        inv = 1.0 / mixed[DV : DV + 1, :]
        linv[head] = jnp.broadcast_to(inv, (8, rows))
        mixed = mixed[:DV, :] * inv
        mixf[head] = mixed
        mixt[pl.ds(pl.multiple_of(head * DV, DV), DV), :] = mixed.astype(BF16)
        return carry

    lax.fori_loop(0, HEADS, forward, 0)
    mb_w = exchange(mixt, mbk, mb_s, mb_r)
    settle(cot_w, 1) if stages > 1 else None
    for k in range(2, stages):
        cot_stage(k)
        if k + 1 < stages:
            settle(cot_w, k)

    dkp[...] = jnp.zeros_like(dkp)

    def backward(head, carry):
        p = pt[head]
        g = (gt[head].astype(F32) * linv[head, :1]).astype(BF16)
        delta = jnp.sum(g.astype(F32) * mixf[head], axis=0, keepdims=True)
        top = (-delta).astype(BF16).astype(F32)
        low = -delta - top
        place = lax.broadcasted_iota(jnp.int32, (256 - DV, rows), 0)
        tail = jnp.where(place == 0, top, jnp.where(place == 1, low, 0.0))
        gl = jnp.concatenate([g, tail.astype(BF16)], axis=0)
        ds = (p.astype(F32) * dot_on(vaug[...], gl, 1, 0)).astype(BF16)
        side = head // (HEADS // 2)
        at = pl.multiple_of(head % (HEADS // 2) * DK, DK)
        gqt[0, side, pl.ds(at, DK), :] = (dot_on(kt[...], ds, 1, 0) * scale).astype(BF16)
        dkp[:, :DK] += dot_on(ds, q[head, :, :DK], 1, 0)
        dkp[:, DK:] += dot_on(p, gl, 1, 1)
        return carry

    gq_w = [[None] * stages for _ in range(2)]
    for h in range(2):
        lax.fori_loop(h * HEADS // 2, (h + 1) * HEADS // 2, backward, 0)
        gq_w[h][0] = gather_stage(gqt, h, 0, gq_s, gq_r)

    def packed(m):
        dk = dkp[m * rows : (m + 1) * rows, :DK] * scale
        dv = dkp[m * rows : (m + 1) * rows, DK : DK + DV]
        return jnp.concatenate(pack(dk, dv), axis=0)

    def halve(k, value, zs, zr, ssem, rsem, waits):
        bit = tbits[k]
        for r in range(nt):
            if r & (2 * bit - 1) == bit:
                zs[r] = value(r).astype(BF16)
                waits[r ^ bit, k] = push(
                    "trunk", flip(trunk, bit), zs.at[r], zr.at[r], ssem.at[r], rsem.at[r]
                )

    def gained(first, zr, waits, upto):
        def value(r):
            out = first(r)
            for k in range(upto):
                waits[r, k].wait_recv()
                out = out + zr[r | tbits[k]].astype(F32)
            return out

        return value

    d_w, o_w, q_w, c_w = {}, {}, {}, {}
    halve(0, packed, zs_d, zr_d, d_s, d_r, d_w)

    nrm[...] = dot_on(mixt[...], wo[...], 0, 0).astype(BF16)
    stores.append(store(1, nrm, upd_o))

    settle(gq_w, 0)
    for h in range(2):
        gq_w[h][1] = gather_stage(gqt, h, 1, gq_s, gq_r)
    for k in range(1, len(tbits)):
        halve(k, gained(packed, zr_d, d_w, k), zs_d, zr_d, d_s, d_r, d_w)

    settle(cot_w, stages - 1)
    for m in range(1, n):
        mb_w[m].wait_recv()
    mbk[0] = mixt[block(seq), :]

    def fetch(m):
        copy = pltpu.make_async_copy(cot.at[m], cbuf.at[1 + m % 2], c_sem.at[m])
        copy.start()
        return copy

    fetched = {m: fetch(m) for m in range(1, min(n, 3))}
    for m in range(n):
        if m:
            fetched[m].wait()
        term = dot_on(mbk[m], cbuf[1 + m % 2 if m else 0].reshape(rows, width), 1, 0)
        product = term if m == 0 else product + term
        if m and m + 2 < n:
            fetched[m + 2] = fetch(m + 2)

    def rows_of(ref):
        return lambda r: ref[flip(trunk, r)]

    def keep(ref, value):
        for t in range(nt):
            ref[t] = value[t * part : (t + 1) * part, :]

    keep(ost, product)
    halve(0, rows_of(ost), zs_o, zr_o, o_s, o_r, o_w)

    grad_context = gained(packed, zr_d, d_w, len(tbits))(0).astype(BF16)
    gcx[0] = grad_context.reshape(gcx.shape[1:])
    gc_w = [[None] * stages for _ in range(2)]
    for h in range(2):
        gc_w[h][0] = gather_stage(gcx, h, 0, gc_s, gc_r)

    if stages > 1:
        settle(gq_w, 1)
    for k in range(2, stages):
        for h in range(2):
            gq_w[h][k] = gather_stage(gqt, h, k, gq_s, gq_r)
        if k + 1 < stages:
            settle(gq_w, k)

    def unpack(m):
        flat = gcx[m].reshape(2 * rows + half, 128)
        tail = flat[2 * rows :, :]
        v1 = jnp.concatenate([tail[:, :64], tail[:, 64:]], axis=0)
        return jnp.concatenate([flat[:rows], flat[rows : 2 * rows], v1], axis=1)

    gq = jnp.concatenate([gqt[0, 0], gqt[0, 1]], axis=0).T
    grad_white = (dot_on(gq, wq[...], 1, 1) + dot_on(unpack(0), wc[...], 1, 0)) * gain[...].reshape(
        1, width
    )
    wide = enc[...].astype(F32)
    inverse = lax.rsqrt(jnp.mean(wide * wide, axis=-1, keepdims=True) + EPS)
    white = wide * inverse
    stores[0].wait()
    enc[...] = (
        inverse * (grad_white - white * jnp.mean(grad_white * white, axis=-1, keepdims=True))
    ).astype(BF16)
    stores.append(store(2, enc, inp_o))
    for k in range(1, len(tbits)):
        halve(k, gained(rows_of(ost), zr_o, o_w, k), zs_o, zr_o, o_s, o_r, o_w)

    for k in range(1, stages):
        settle(gc_w, k - 1)
        for h in range(2):
            gc_w[h][k] = gather_stage(gcx, h, k, gc_s, gc_r)

    for m in range(1, n):
        nb_w[m].wait_recv()
    nbk[0] = nrt[block(seq), :]
    settle(gq_w, stages - 1)
    sides = []
    for h in range(2):
        for m in range(n):
            term = dot_on(nbk[m], gqt[m, h], 1, 1)
            product = term if m == 0 else product + term
        sides.append(product)
    keep(qst, jnp.concatenate(sides, axis=1))
    halve(0, rows_of(qst), zs_q, zr_q, qz_s, qz_r, q_w)

    settle(gc_w, stages - 1)
    for m in range(n):
        term = dot_on(nbk[m], unpack(m), 1, 0)
        product = term if m == 0 else product + term
    keep(cst, product)
    halve(0, rows_of(cst), zs_c, zr_c, cz_s, cz_r, c_w)

    for k in range(1, len(tbits)):
        halve(k, gained(rows_of(qst), zr_q, q_w, k), zs_q, zr_q, qz_s, qz_r, q_w)
        halve(k, gained(rows_of(cst), zr_c, c_w, k), zs_c, zr_c, cz_s, cz_r, c_w)
    og[...] = gained(rows_of(ost), zr_o, o_w, len(tbits))(0) * factor
    stores.append(store(3, og, og_o))
    qg[...] = gained(rows_of(qst), zr_q, q_w, len(tbits))(0) * factor
    stores.append(store(4, qg, qg_o))
    cg[...] = gained(rows_of(cst), zr_c, c_w, len(tbits))(0) * factor
    stores.append(store(5, cg, cg_o))

    for copy in sends:
        copy.wait_send()
    for copy in stores[1:]:
        copy.wait()


def finish_kernel(count, *refs):
    sources, results, held = refs[:count], refs[count : 2 * count], refs[2 * count : 3 * count]
    in_sem, out_sem = refs[3 * count :]
    reads = [
        pltpu.make_async_copy(sources[i], held[i], in_sem.at[i]) for i in range(count)
    ]
    writes = [
        pltpu.make_async_copy(held[i], results[i], out_sem.at[i]) for i in range(count)
    ]
    for copy in reads:
        copy.start()
    for read, write in zip(reads, writes):
        read.wait()
        write.start()
    for copy in writes:
        copy.wait()


def finish(arrays):
    count = len(arrays)
    anywhere = pl.BlockSpec(memory_space=pl.ANY)
    return pl.pallas_call(
        functools.partial(finish_kernel, count),
        out_shape=tuple(jax.ShapeDtypeStruct(a.shape, a.dtype) for a in arrays),
        in_specs=[anywhere] * count,
        out_specs=[anywhere] * count,
        scratch_shapes=[pltpu.VMEM(a.shape, a.dtype) for a in arrays]
        + [pltpu.SemaphoreType.DMA((count,))] * 2,
        compiler_params=pltpu.CompilerParams(vmem_limit_bytes=67043328),
    )(*arrays)


def body(
    tokens,
    first_weight,
    second_weight,
    third_weight,
    norm_gain,
    query_weight,
    context_weight,
    output_weight,
    pair_bias,
    cotangent,
):
    n, nt = lax.axis_size("seq"), lax.axis_size("trunk")
    rows, width = cotangent.shape[1:]
    taps, c1 = first_weight.shape
    total = nt * rows
    blocks = pair_bias.shape[3]
    half = rows // 2
    blk = width // n
    part = blk // nt
    flat = 2 * rows + half
    tokens = tokens.reshape(rows, tokens.shape[1] // rows)
    vm = pltpu.VMEM
    dma = pltpu.SemaphoreType.DMA
    shape = jax.ShapeDtypeStruct
    out_shape = (
        shape((rows, width), BF16),
        shape((rows, width), BF16),
        shape((rows, width), BF16),
        shape((part, HEADS * DK), F32),
        shape((part, DK + DV), F32),
        shape((part, width), F32),
        shape((n, 2, half, width), BF16),
    )
    zed = lambda *dims: [vm((nt,) + dims, BF16), vm((nt,) + dims, BF16)]
    scratch = [
        vm(tokens.shape, jnp.int32),
        vm(first_weight.shape, BF16),
        vm(second_weight.shape, BF16),
        vm(third_weight.shape, BF16),
        vm((width,), F32),
        vm((DK + DV, width), BF16),
        vm(pair_bias.shape[1:], F32),
        vm((rows, width), BF16),
        vm((rows, width), BF16),
        vm((width, rows), BF16),
        vm((n, blk, rows), BF16),
        vm((HEADS, rows, DK + 2 * blocks), BF16),
        vm((HEADS, DV, rows), BF16),
        vm((nt, flat, 128), BF16),
        vm((total, DK + 2 * blocks), BF16),
        vm((DK, total), BF16),
        vm((total, 256), BF16),
        vm((256, total), BF16),
        vm((HEADS, total, rows), BF16),
        vm((HEADS, 8, rows), F32),
        vm((width, rows), BF16),
        vm((HEADS, DV, rows), F32),
        vm((n, blk, rows), BF16),
        vm((3, 2, half, width), BF16),
        vm((n, 2, HEADS // 2 * DK, rows), BF16),
        vm((n, 2, flat // 2, 128), BF16),
        vm((total, DK + 256), F32),
        vm((nt, part, width), F32),
        vm((nt, part, HEADS * DK), F32),
        vm((nt, part, DK + DV), F32),
        *zed(flat, 128),
        *zed(part, width),
        *zed(part, HEADS * DK),
        *zed(part, DK + DV),
        vm((part, HEADS * DK), F32),
        vm((part, DK + DV), F32),
        vm((part, width), F32),
        dma((10,)),
        dma((6,)),
        dma((n,)),
        dma((2, n)), dma((2, n)),
        dma((nt,)), dma((nt,)),
        dma((n,)), dma((n,)),
        dma((n,)), dma((n,)),
        dma((2, n)), dma((2, n)),
        dma((2, n)), dma((2, n)),
        dma((nt,)), dma((nt,)),
        dma((nt,)), dma((nt,)),
        dma((nt,)), dma((nt,)),
        dma((nt,)), dma((nt,)),
    ]
    anywhere = pl.BlockSpec(memory_space=pl.ANY)
    *results, _ = pl.pallas_call(
        functools.partial(kernel, n, nt),
        out_shape=out_shape,
        in_specs=[anywhere] * 10,
        out_specs=[anywhere] * 7,
        scratch_shapes=scratch,
        compiler_params=pltpu.CompilerParams(
            collective_id=0, has_side_effects=True, vmem_limit_bytes=67043328
        ),
    )(
        tokens,
        first_weight,
        second_weight,
        third_weight,
        norm_gain,
        query_weight,
        context_weight.T,
        output_weight,
        pair_bias[0],
        cotangent[0],
    )
    encoded, update, input_gradient, qg, cg, og = finish(results)
    return (
        encoded.reshape(1, rows, width),
        update.reshape(1, rows, width),
        input_gradient.reshape(1, rows, width),
        qg,
        cg,
        og,
    )


def solution(mesh):
    placed = (
        P("seq", "trunk"),
        P(),
        P(),
        P(),
        P(),
        P(),
        P(),
        P(),
        P("seq", None, "trunk", None),
        P("seq", "trunk", None),
    )
    return jax.shard_map(
        body,
        mesh=mesh,
        in_specs=placed,
        out_specs=(
            P("seq", "trunk", None),
            P("seq", "trunk", None),
            P("seq", "trunk", None),
            P(("seq", "trunk"), None),
            P(("seq", "trunk"), None),
            P(("seq", "trunk"), None),
        ),
        check_vma=False,
    )
```
